128 devices in a mesh: energy: 16 (over z, y_hi, core), layer: 8 (over y_lo, x).
Axes of the slice: x: 4, y: 4 (y_hi: 2, y_lo: 2; y = y_hi * 2 + y_lo), z: 4, core: 2. Of those that a mesh axis runs over, the one named last changes fastest.
Arguments:
- green_local: bfloat16 [8, 32, 384, 2, 384], P('layer', 'energy'), may hold values from -6 to 6
- hopping: bfloat16 [8, 384, 2, 384], P('layer'), may hold values from -0.005859375 to 0.005859375
- coupling: bfloat16 [8, 384, 384], P('layer'), may hold values from -0.25 to 0.25
Outputs:
- green_full: bfloat16 [8, 32, 384, 2, 384], P('layer', 'energy')
The draws below stay inside these ranges and needn't reach their ends.
All inputs are finite; a program needn't handle non-finite values.
Results may differ from the reference program's by a relative error of at most 0.02.
Values may be sent and summed in bfloat16 or wider, within the bound.
No kernel may reach another device: no remote copies, remote signals or barrier semaphores. Data moves between devices by JAX's collectives and lax.ppermute only.
A program may use at most 64 MiB of HBM per device.

```python
import jax
import jax.numpy as jnp
from jax import lax

ORB = 384
OFFSET = 2
ENERGIES = 32
LAYERS = 8


def block_scale(key, dims, shards, smallest, largest):
    def one(dim, shards_of):
        steps = jax.random.uniform(jax.random.fold_in(jax.random.fold_in(key, 6), dim), (shards_of,), jnp.float32, smallest / len(shards), largest / len(shards))
        return jnp.repeat(jnp.exp(steps), dims[dim] // shards_of).reshape((-1,) + (1,) * (len(dims) - dim - 1))

    factor_of = one(*shards[0])
    for cut in shards[1:]:
        factor_of = factor_of * one(*cut)
    return factor_of


def centred(own_key, extent, spread, most, cuts=(), dtype=jnp.bfloat16):
    factor_of = block_scale(own_key, extent, cuts, -0.22, 0.18) if cuts else 1.0
    entries = jax.random.normal(own_key, extent, jnp.float32) * spread * factor_of
    return jnp.minimum(jnp.maximum(entries, -most), most).astype(dtype)


def setup_inputs(seed: int = 0) -> dict:
    streams_of = jax.random.split(jax.random.key(seed), 4)
    return {
        "green_local": centred(streams_of[0], (LAYERS, ENERGIES, ORB, 2, ORB), 1.0, 6.0, ((0, 8), (1, 16))),
        "hopping": centred(streams_of[1], (LAYERS, ORB, 2, ORB), (ORB * ORB * 19 // 3) ** -0.5, 0.005859375, ((0, 8),)),
        "coupling": centred(streams_of[2], (LAYERS, ORB, ORB), (ORB * 7 // 5) ** -0.5, 0.25, ((0, 8),)),
    }


def expand(blocks):
    real_part = blocks[..., :, 0, :]
    imag_part = blocks[..., :, 1, :]
    upper_half = jnp.concatenate([real_part, imag_part], axis=-1)
    lower_half = jnp.concatenate([-imag_part, real_part], axis=-1)
    return jnp.concatenate([upper_half, lower_half], axis=-2)


def complex_product(left_block, right_block):
    row_blocks = left_block.astype(jnp.float32).reshape(left_block.shape[:-2] + (2 * left_block.shape[-1],))
    product_rows = jnp.matmul(row_blocks, expand(right_block.astype(jnp.float32)), precision=lax.Precision.HIGHEST)
    return product_rows.reshape(left_block.shape)


def partner_sum(following):
    padded = jnp.pad(following.astype(jnp.float32), ((OFFSET, OFFSET), (0, 0), (0, 0), (0, 0)))
    count = following.shape[0]
    return (padded[2 * OFFSET:] + padded[:count]).astype(jnp.bfloat16)


def reference(green_local, hopping, coupling):
    layer_count = green_local.shape[0]
    following = green_local[layer_count - 1]
    results = [None] * layer_count
    for layer_index in range(layer_count - 1, -1, -1):
        isolated = green_local[layer_index]
        phonon = coupling[layer_index].astype(jnp.float32)
        coupled = complex_product(isolated, hopping[layer_index]).astype(jnp.bfloat16)
        partner = partner_sum(following)
        scatter_left = jnp.einsum("ij,ejcl->eicl", phonon, partner.astype(jnp.float32), precision=lax.Precision.HIGHEST).astype(jnp.bfloat16)
        combined = (following.astype(jnp.float32) + jnp.matmul(scatter_left.astype(jnp.float32), phonon.T, precision=lax.Precision.HIGHEST)).astype(jnp.bfloat16)
        product = complex_product(coupled, combined).astype(jnp.bfloat16)
        flipped = jnp.transpose(coupled, (0, 3, 2, 1))
        following = (isolated.astype(jnp.float32) + complex_product(product, flipped)).astype(jnp.bfloat16)
        results[layer_index] = following
    return jnp.stack(results)
```

```python
import jax
import jax.numpy as jnp
from jax import lax
from jax.experimental import pallas as pl
from jax.experimental.pallas import tpu as pltpu
from jax.sharding import PartitionSpec as P

AXES = ("energy", "layer")
COLUMN = (6, 4)
BF = jnp.bfloat16
F32 = jnp.float32
VM = pl.BlockSpec(memory_space=pltpu.VMEM)
SM = pl.BlockSpec(memory_space=pltpu.SMEM)


def dot(a, b):
    return jnp.dot(a, b, preferred_element_type=F32)


def expanded(block):
    n = block.shape[0]
    return jnp.concatenate([block, jnp.concatenate([-block[:, n:], block[:, :n]], axis=1)], axis=0)


def prepare_kernel(core, isolated, own, other, c_ref, w_ref, d_ref, dt_ref):
    n = isolated.shape[0]
    first = core[0] == 0
    half0 = jnp.where(first, own[...], other[...])
    half1 = jnp.where(first, other[...], own[...])
    both = jnp.concatenate([half0, half1], axis=0)
    hopping, packed = both[:n], both[n:]
    coupled = dot(isolated[...], expanded(hopping)).astype(BF)
    c_ref[...] = coupled
    real_t = coupled[:, :n].T
    imag_t = coupled[:, n:].T
    w_ref[:n, :n] = real_t
    w_ref[:n, n:] = imag_t
    w_ref[n:, :n] = -imag_t
    w_ref[n:, n:] = real_t
    phonon = jnp.concatenate([packed[:, :n], packed[:, n:]], axis=0)
    d_ref[...] = phonon
    dt_ref[...] = phonon.T


def prepare(core, isolated, own, other):
    n = isolated.shape[0]
    shapes = [(n, 2 * n), (2 * n, 2 * n), (n, n), (n, n)]
    return pl.pallas_call(
        prepare_kernel,
        out_shape=[jax.ShapeDtypeStruct(s, BF) for s in shapes],
        in_specs=[SM, VM, VM, VM],
        out_specs=[VM] * 4,
        compiler_params=pltpu.CompilerParams(vmem_limit_bytes=24 << 20),
        cost_estimate=pl.CostEstimate(flops=8 * n**3, bytes_accessed=20 * n * n, transcendentals=0),
    )(core, isolated, own, other)


def advance_kernel(linked, following, near, far, isolated, c_ref, w_ref, d_ref, dt_ref, out):
    n = isolated.shape[0]
    outside = jnp.where(linked[0] != 0, far[...].astype(F32), 0.0)
    partner = (near[...].astype(F32) + outside).astype(BF)
    left = dot(d_ref[...], partner).astype(BF)
    combined_real = (following[:, :n].astype(F32) + dot(left[:, :n], dt_ref[...])).astype(BF)
    combined_imag = (following[:, n:].astype(F32) + dot(left[:, n:], dt_ref[...])).astype(BF)
    combined = jnp.concatenate([combined_real, combined_imag], axis=1)
    product = dot(c_ref[...], expanded(combined)).astype(BF)
    out[...] = (isolated[...].astype(F32) + dot(product, w_ref[...])).astype(BF)


def advance(linked, following, near, far, isolated, prepared):
    n = isolated.shape[0]
    return pl.pallas_call(
        advance_kernel,
        out_shape=jax.ShapeDtypeStruct((n, 2 * n), BF),
        in_specs=[SM] + [VM] * 8,
        out_specs=VM,
        compiler_params=pltpu.CompilerParams(vmem_limit_bytes=24 << 20),
        cost_estimate=pl.CostEstimate(flops=24 * n**3, bytes_accessed=24 * n * n, transcendentals=0),
    )(linked, following, near, far, isolated, *prepared)


def after(value, *others):
    return lax.optimization_barrier((value, *others))[0]


def make(energies, layers):
    def device(k, j):
        return (k % energies) * layers + j

    def seat(k, p):
        return device(k, COLUMN[p])

    chip_swap = [(device(k, j), device(k ^ 1, j)) for k in range(energies) for j in range(layers)]

    def far_swap():
        pairs = []
        for k in range(energies):
            other = k + 1 if k % 2 else k - 1
            for j in range(layers):
                if j in COLUMN:
                    p = COLUMN.index(j)
                    pairs.append((seat(k, p), seat(other, p)))
                else:
                    pairs.append((device(k, j), device(k ^ 1, j)))
        return pairs

    far_pairs = far_swap()

    def to_seat(l, p):
        return [(device(k, l), seat(k, p)) for k in range(energies)]

    def to_home(l, p):
        return [(seat(k, p), device(k, l)) for k in range(energies)]

    def per_device(green_local, hopping, coupling):
        k = lax.axis_index("energy")
        core = (k % 2).astype(jnp.int32)
        linked = jnp.where((k == 0) | (k == energies - 1), 0, 1).astype(jnp.int32).reshape(1)
        n = hopping.shape[1]
        isolated = [green_local[0, p].reshape(n, 2 * n) for p in range(2)]
        coupling_rows = jnp.concatenate([coupling[0, : n // 2], coupling[0, n // 2 :]], axis=1)
        shared = jnp.concatenate([hopping[0].reshape(n, 2 * n), coupling_rows], axis=0)
        half = shared.shape[0] // 2
        my_half = lax.dynamic_slice_in_dim(shared, core * half, half, axis=0)
        core = core.reshape(1)

        def move(value, pairs):
            return lax.ppermute(value, AXES, pairs)

        def fetch(l, token=None):
            green = [after(g, token) if token is not None else g for g in isolated]
            mine = after(my_half, token) if token is not None else my_half
            blocks = move(green[0], to_seat(l, 0)) + move(green[1], to_seat(l, 1))
            halves = move(mine, to_seat(l, 0)) + move(mine, to_seat(l, 1))
            return blocks, halves

        depth = 2
        top = layers - 1
        fetched = {l: fetch(l) for l in range(top, top - depth, -1)}
        following = fetched[top][0]
        back = [jnp.zeros((n, 2 * n), BF)] * 2
        for l in range(top, -1, -1):
            near = move(following, chip_swap)
            far = move(following, far_pairs)
            if l - depth >= 0:
                fetched[l - depth] = fetch(l - depth, following)
            block, own = fetched.pop(l)
            own = after(own, following)
            other = move(own, chip_swap)
            prepared = prepare(core, block, own, other)
            following = advance(linked, following, near, far, block, prepared)
            for p in range(2):
                back[p] = back[p] + move(following, to_home(l, p))
        return jnp.stack([b.reshape(n, 2, n) for b in back])[None]

    return per_device


def solution(mesh):
    placed = (
        P("layer", "energy", None, None, None),
        P("layer", None, None, None),
        P("layer", None, None),
    )
    return jax.shard_map(
        make(mesh.shape["energy"], mesh.shape["layer"]),
        mesh=mesh,
        in_specs=placed,
        out_specs=P("layer", "energy", None, None, None),
        check_vma=False,
    )
```

```python
import jax
import jax.numpy as jnp
from jax import lax
from jax.experimental import pallas as pl
from jax.experimental.pallas import tpu as pltpu
from jax.sharding import PartitionSpec as P

AXES = ("energy", "layer")
BF = jnp.bfloat16
F32 = jnp.float32
VM = pl.BlockSpec(memory_space=pltpu.VMEM)
SM = pl.BlockSpec(memory_space=pltpu.SMEM)


def dot(a, b):
    return jnp.dot(a, b, preferred_element_type=F32)


def expanded(block):
    n = block.shape[0]
    return jnp.concatenate([block, jnp.concatenate([-block[:, n:], block[:, :n]], axis=1)], axis=0)


def prepare_kernel(core, pack, own, other, c_ref, w_ref, d_ref, dt_ref):
    n = d_ref.shape[0]
    first = core[0] == 0
    half0 = jnp.where(first, own[...], other[...])
    half1 = jnp.where(first, other[...], own[...])
    both = jnp.concatenate([half0, half1], axis=0)
    hopping, packed = both[:n], both[n:]
    coupled = dot(pack[:n], expanded(hopping)).astype(BF)
    c_ref[...] = coupled
    real_t = coupled[:, :n].T
    imag_t = coupled[:, n:].T
    w_ref[:n, :n] = real_t
    w_ref[:n, n:] = imag_t
    w_ref[n:, :n] = -imag_t
    w_ref[n:, n:] = real_t
    phonon = jnp.concatenate([packed[:, :n], packed[:, n:]], axis=0)
    d_ref[...] = phonon
    dt_ref[...] = phonon.T


def prepare(core, pack, own, other):
    n = pack.shape[1] // 2
    shapes = [(n, 2 * n), (2 * n, 2 * n), (n, n), (n, n)]
    return pl.pallas_call(
        prepare_kernel,
        out_shape=[jax.ShapeDtypeStruct(s, BF) for s in shapes],
        in_specs=[SM, VM, VM, VM],
        out_specs=[VM] * 4,
        compiler_params=pltpu.CompilerParams(vmem_limit_bytes=24 << 20),
        cost_estimate=pl.CostEstimate(flops=8 * n**3, bytes_accessed=20 * n * n, transcendentals=0),
    )(core, pack, own, other)


def advance_kernel(linked, following, near, far, pack, c_ref, w_ref, d_ref, dt_ref, out):
    n = out.shape[0]
    outside = jnp.where(linked[0] != 0, far[...].astype(F32), 0.0)
    partner = (near[...].astype(F32) + outside).astype(BF)
    left = dot(d_ref[...], partner).astype(BF)
    combined_real = (following[:, :n].astype(F32) + dot(left[:, :n], dt_ref[...])).astype(BF)
    combined_imag = (following[:, n:].astype(F32) + dot(left[:, n:], dt_ref[...])).astype(BF)
    combined = jnp.concatenate([combined_real, combined_imag], axis=1)
    product = dot(c_ref[...], expanded(combined)).astype(BF)
    out[...] = (pack[:n].astype(F32) + dot(product, w_ref[...])).astype(BF)


def advance(linked, following, near, far, pack, prepared):
    n = following.shape[0]
    return pl.pallas_call(
        advance_kernel,
        out_shape=jax.ShapeDtypeStruct((n, 2 * n), BF),
        in_specs=[SM] + [VM] * 8,
        out_specs=VM,
        compiler_params=pltpu.CompilerParams(vmem_limit_bytes=24 << 20),
        cost_estimate=pl.CostEstimate(flops=24 * n**3, bytes_accessed=24 * n * n, transcendentals=0),
    )(linked, following, near, far, pack, *prepared)


def after(value, *others):
    return lax.optimization_barrier((value, *others))[0]


def device(x, y, z, core):
    return ((z * 2 + y // 2) * 2 + core) * 8 + (y % 2) * 4 + x


SEATS = (
    [((3, 2)[(i // 2 + i) % 2], 1 + 2 * (i % 2), i // 2) for i in range(8)],
    [((1, 0)[(i // 2 + i) % 2], 1 + 2 * (i % 2), i // 2) for i in range(8)],
)
DEPTH = 2


def make(energies, layers):
    def home(k, l):
        return k * layers + l

    def seat(k, p):
        k %= energies
        return device(*SEATS[p][k // 2], k % 2)

    chip_swap = [(home(k, j), home(k ^ 1, j)) for k in range(energies) for j in range(layers)]
    far_pairs = {}
    for p in range(2):
        for k in range(energies):
            far_pairs[seat(k, p)] = seat(k + 1 if k % 2 else k - 1, p)
    far_pairs = [(s, far_pairs.get(s, d)) for s, d in chip_swap]
    top = layers - 1

    def to_seat(l, p):
        return [(home(k, l), seat(k, p)) for k in range(energies)] if 0 <= l <= top else []

    def to_home(l, p):
        return [(t, s) for s, t in to_seat(l, p)]

    def per_device(green_local, hopping, coupling):
        k = lax.axis_index("energy")
        position = lax.axis_index("layer")
        core = (k % 2).astype(jnp.int32)
        n = hopping.shape[1]
        me = k * layers + position
        ends = [me == seat(e, p) for e in (0, energies - 1) for p in range(2)]
        linked = jnp.where(ends[0] | ends[1] | ends[2] | ends[3], 0, 1).astype(jnp.int32).reshape(1)
        isolated = [green_local[0, p].reshape(n, 2 * n) for p in range(2)]
        coupling_rows = jnp.concatenate([coupling[0, : n // 2], coupling[0, n // 2 :]], axis=1)
        shared = jnp.concatenate([hopping[0].reshape(n, 2 * n), coupling_rows], axis=0)
        half = shared.shape[0] // 2
        my_half = lax.dynamic_slice_in_dim(shared, core * half, half, axis=0)
        core = core.reshape(1)

        def move(value, pairs):
            return lax.ppermute(value, AXES, pairs)

        even = (top - position) % 2 == 0
        first = move(isolated[0], to_seat(top, 0)) + move(isolated[1], to_seat(top, 1))
        halves = move(after(my_half, *isolated), to_seat(top, 0))
        blocks = [jnp.where(even, isolated[0], isolated[1]), jnp.where(even, isolated[1], isolated[0])]
        packs = [jnp.concatenate([b, my_half], axis=0) for b in blocks]
        arrived = {}

        def fetch(s, token):
            pairs = to_seat(top - s, 0) + to_seat(top + 1 - s, 1)
            arrived[s] = move(after(packs[s % 2], token), pairs)

        following = first
        for s in range(1, DEPTH):
            fetch(s, first)
        back = [[], []]
        for s in range(layers + 1):
            far = move(following, far_pairs)
            near = move(following, chip_swap)
            if s > 0:
                pairs = to_home(top + 1 - s, 0) + to_home(top + 2 - s, 1)
                back[(s - 1) % 2].append(move(following, pairs))
            if DEPTH <= s + DEPTH <= layers:
                fetch(s + DEPTH, following)
            if s == 0:
                pack, own = first, halves
            else:
                pack = after(arrived.pop(s), following)
                own = pack[n:]
            other = move(own, chip_swap)
            prepared = prepare(core, pack, own, other)
            if s > 2:
                waiting = back[(s - 1) % 2]
                if len(waiting) > 1:
                    done = waiting.pop(0)
                    waiting[0:0] = []
                    held = sums[(s - 1) % 2]
                    sums[(s - 1) % 2] = done if held is None else held + done
                    far = after(far, sums[(s - 1) % 2])
            else:
                sums = [None, None]
            following = advance(linked, following, near, far, pack, prepared)
        pairs = to_home(0, 1)
        back[layers % 2].append(move(following, pairs))
        totals = []
        for held, parts in zip(sums, back, strict=True):
            for part in parts:
                held = part if held is None else held + part
            totals.append(held)
        result = [jnp.where(even, totals[p], totals[1 - p]) for p in range(2)]
        return jnp.stack([r.reshape(n, 2, n) for r in result])[None]

    return per_device


def solution(mesh):
    placed = (
        P("layer", "energy", None, None, None),
        P("layer", None, None, None),
        P("layer", None, None),
    )
    return jax.shard_map(
        make(mesh.shape["energy"], mesh.shape["layer"]),
        mesh=mesh,
        in_specs=placed,
        out_specs=P("layer", "energy", None, None, None),
        check_vma=False,
    )
```

```python
import jax
import jax.numpy as jnp
from jax import lax
from jax.experimental import pallas as pl
from jax.experimental.pallas import tpu as pltpu
from jax.sharding import PartitionSpec as P

AXES = ("energy", "layer")
BF = jnp.bfloat16
F32 = jnp.float32
VM = pl.BlockSpec(memory_space=pltpu.VMEM)
SM = pl.BlockSpec(memory_space=pltpu.SMEM)


def dot(a, b):
    return jnp.dot(a, b, preferred_element_type=F32)


def expanded(block):
    n = block.shape[0]
    return jnp.concatenate([block, jnp.concatenate([-block[:, n:], block[:, :n]], axis=1)], axis=0)


def prepare_kernel(core, pack, own, other, c_ref, w_ref, d_ref, dt_ref):
    n = d_ref.shape[0]
    first = core[0] == 0
    half0 = jnp.where(first, own[...], other[...])
    half1 = jnp.where(first, other[...], own[...])
    both = jnp.concatenate([half0, half1], axis=0)
    hopping, packed = both[:n], both[n:]
    coupled = dot(pack[:n], expanded(hopping)).astype(BF)
    c_ref[...] = coupled
    real_t = coupled[:, :n].T
    imag_t = coupled[:, n:].T
    w_ref[:n, :n] = real_t
    w_ref[:n, n:] = imag_t
    w_ref[n:, :n] = -imag_t
    w_ref[n:, n:] = real_t
    phonon = jnp.concatenate([packed[:, :n], packed[:, n:]], axis=0)
    d_ref[...] = phonon
    dt_ref[...] = phonon.T


def prepare(core, pack, own, other):
    n = pack.shape[1] // 2
    shapes = [(n, 2 * n), (2 * n, 2 * n), (n, n), (n, n)]
    return pl.pallas_call(
        prepare_kernel,
        out_shape=[jax.ShapeDtypeStruct(s, BF) for s in shapes],
        in_specs=[SM, VM, VM, VM],
        out_specs=[VM] * 4,
        compiler_params=pltpu.CompilerParams(vmem_limit_bytes=24 << 20),
        cost_estimate=pl.CostEstimate(flops=8 * n**3, bytes_accessed=20 * n * n, transcendentals=0),
    )(core, pack, own, other)


def advance_kernel(linked, following, near, far, pack, c_ref, w_ref, d_ref, dt_ref, out):
    n = out.shape[0]
    outside = jnp.where(linked[0] != 0, far[...].astype(F32), 0.0)
    partner = (near[...].astype(F32) + outside).astype(BF)
    left = dot(d_ref[...], partner).astype(BF)
    combined_real = (following[:, :n].astype(F32) + dot(left[:, :n], dt_ref[...])).astype(BF)
    combined_imag = (following[:, n:].astype(F32) + dot(left[:, n:], dt_ref[...])).astype(BF)
    combined = jnp.concatenate([combined_real, combined_imag], axis=1)
    product = dot(c_ref[...], expanded(combined)).astype(BF)
    out[...] = (pack[:n].astype(F32) + dot(product, w_ref[...])).astype(BF)


def advance(linked, following, near, far, pack, prepared):
    n = following.shape[0]
    return pl.pallas_call(
        advance_kernel,
        out_shape=jax.ShapeDtypeStruct((n, 2 * n), BF),
        in_specs=[SM] + [VM] * 8,
        out_specs=VM,
        compiler_params=pltpu.CompilerParams(vmem_limit_bytes=24 << 20),
        cost_estimate=pl.CostEstimate(flops=24 * n**3, bytes_accessed=24 * n * n, transcendentals=0),
    )(linked, following, near, far, pack, *prepared)


def after(value, *others):
    return lax.optimization_barrier((value, *others))[0]


def device(x, y, z, core):
    return ((z * 2 + y // 2) * 2 + core) * 8 + (y % 2) * 4 + x


PLACES = ([(0, 1), (0, 2), (0, 0), (0, 3)], [(2, 0), (2, 3), (2, 1), (2, 2)])
SEATS = [[(*place[i % 4], i // 2) for i in range(8)] for place in PLACES]
DEPTH = 5


def make(energies, layers):
    def home(k, l):
        return k * layers + l

    def seat(k, p):
        k %= energies
        return device(*SEATS[p][k // 2], k % 2)

    chip_swap = [(home(k, j), home(k ^ 1, j)) for k in range(energies) for j in range(layers)]
    far_pairs = {}
    for p in range(2):
        for k in range(energies):
            far_pairs[seat(k, p)] = seat(k + 1 if k % 2 else k - 1, p)
    far_pairs = [(s, far_pairs.get(s, d)) for s, d in chip_swap]
    top = layers - 1

    def to_seat(l, p):
        return [(home(k, l), seat(k, p)) for k in range(energies)] if 0 <= l <= top else []

    def to_home(l, p):
        return [(t, s) for s, t in to_seat(l, p)]

    def per_device(green_local, hopping, coupling):
        k = lax.axis_index("energy")
        position = lax.axis_index("layer")
        core = (k % 2).astype(jnp.int32)
        n = hopping.shape[1]
        me = k * layers + position
        ends = [me == seat(e, p) for e in (0, energies - 1) for p in range(2)]
        linked = jnp.where(ends[0] | ends[1] | ends[2] | ends[3], 0, 1).astype(jnp.int32).reshape(1)
        isolated = [green_local[0, p].reshape(n, 2 * n) for p in range(2)]
        coupling_rows = jnp.concatenate([coupling[0, : n // 2], coupling[0, n // 2 :]], axis=1)
        shared = jnp.concatenate([hopping[0].reshape(n, 2 * n), coupling_rows], axis=0)
        half = shared.shape[0] // 2
        my_half = lax.dynamic_slice_in_dim(shared, core * half, half, axis=0)
        core = core.reshape(1)

        def move(value, pairs):
            return lax.ppermute(value, AXES, pairs)

        even = (top - position) % 2 == 0
        first = move(isolated[0], to_seat(top, 0))
        halves = move(my_half, to_seat(top, 0))
        blocks = [jnp.where(even, isolated[0], isolated[1]), jnp.where(even, isolated[1], isolated[0])]
        packs = [jnp.concatenate([b, my_half], axis=0) for b in blocks]
        arrived = {}

        def fetch(s, token):
            pairs = to_seat(top - s, 0) + to_seat(top + 1 - s, 1)
            arrived[s] = move(after(packs[s % 2], token), pairs)

        second_chain = me == seat(0, 1)
        for e in range(1, energies):
            second_chain |= me == seat(e, 1)
        following = first
        fetch(1, my_half)
        for s in range(2, DEPTH):
            fetch(s, first)
        waiting, sums = [[], []], [None, None]
        for s in range(layers + 1):
            if s == 0:
                pack, own = first, halves
            elif s == 1:
                pack = after(arrived.pop(s), following)
                own = pack[n:]
                result_0 = following
                following = jnp.where(second_chain, pack[:n], following)
            else:
                pack = after(arrived.pop(s), following)
                own = pack[n:]
            far = move(following, far_pairs)
            near = move(following, chip_swap)
            if s > 0:
                pairs = to_home(top + 1 - s, 0) + to_home(top + 2 - s, 1)
                waiting[(s - 1) % 2].append(move(result_0 if s == 1 else following, pairs))
            if s + DEPTH <= layers:
                fetch(s + DEPTH, following)
            other = move(own, chip_swap)
            prepared = prepare(core, pack, own, other)
            following = advance(linked, following, near, far, pack, prepared)
            if s > 2:
                i = (s - 1) % 2
                part = after(waiting[i].pop(0), following)
                sums[i] = part if sums[i] is None else sums[i] + part
        waiting[layers % 2].append(move(following, to_home(0, 1)))
        totals = []
        for held, parts in zip(sums, waiting, strict=True):
            for part in parts:
                held = part if held is None else held + part
            totals.append(held)
        result = [jnp.where(even, totals[p], totals[1 - p]) for p in range(2)]
        return jnp.stack([r.reshape(n, 2, n) for r in result])[None]

    return per_device


def solution(mesh):
    placed = (
        P("layer", "energy", None, None, None),
        P("layer", None, None, None),
        P("layer", None, None),
    )
    return jax.shard_map(
        make(mesh.shape["energy"], mesh.shape["layer"]),
        mesh=mesh,
        in_specs=placed,
        out_specs=P("layer", "energy", None, None, None),
        check_vma=False,
    )
```

```python
import jax
import jax.numpy as jnp
from jax import lax
from jax.experimental import pallas as pl
from jax.experimental.pallas import tpu as pltpu
from jax.sharding import PartitionSpec as P

AXES = ("energy", "layer")
BF = jnp.bfloat16
BLOCK = 128
ROWS = 192
F32 = jnp.float32
VM = pl.BlockSpec(memory_space=pltpu.VMEM)
SM = pl.BlockSpec(memory_space=pltpu.SMEM)


def dot(a, b):
    return jnp.dot(a, b, preferred_element_type=F32)


def expanded(block):
    n = block.shape[0]
    return jnp.concatenate([block, jnp.concatenate([-block[:, n:], block[:, :n]], axis=1)], axis=0)


def prepare_kernel(core, pack, own, other, c_ref, w_ref, d_ref, dt_ref, right):
    n = d_ref.shape[0]
    first = core[0] == 0
    half0 = jnp.where(first, own[...], other[...])
    half1 = jnp.where(first, other[...], own[...])
    both = jnp.concatenate([half0, half1], axis=0)
    hopping, packed = both[:n], both[n:]
    right[...] = expanded(hopping)

    @pl.loop(0, n // BLOCK)
    def _(i):
        here = pl.multiple_of(i * BLOCK, BLOCK)
        rows, after_rows = pl.ds(here, BLOCK), pl.ds(pl.multiple_of(n + here, BLOCK), BLOCK)
        coupled = dot(pack[rows, :], right[...]).astype(BF)
        c_ref[rows, :] = coupled
        real_t = coupled[:, :n].T
        imag_t = coupled[:, n:].T
        w_ref[:n, rows] = real_t
        w_ref[:n, after_rows] = imag_t
        w_ref[n:, rows] = -imag_t
        w_ref[n:, after_rows] = real_t

    phonon = jnp.concatenate([packed[:, :n], packed[:, n:]], axis=0)
    d_ref[...] = phonon
    dt_ref[...] = phonon.T


def prepare(core, pack, own, other):
    n = pack.shape[1] // 2
    shapes = [(n, 2 * n), (2 * n, 2 * n), (n, n), (n, n)]
    return pl.pallas_call(
        prepare_kernel,
        out_shape=[jax.ShapeDtypeStruct(s, BF) for s in shapes],
        in_specs=[SM, VM, VM, VM],
        out_specs=[VM] * 4,
        scratch_shapes=[pltpu.VMEM((2 * n, 2 * n), BF)],
        compiler_params=pltpu.CompilerParams(vmem_limit_bytes=24 << 20),
        cost_estimate=pl.CostEstimate(flops=8 * n**3, bytes_accessed=20 * n * n, transcendentals=0),
    )(core, pack, own, other)


def advance_kernel(linked, following, near, far, pack, c_ref, w_ref, d_ref, dt_ref, out, right):
    n = out.shape[0]
    outside = jnp.where(linked[0] != 0, far[...].astype(F32), 0.0)
    partner = (near[...].astype(F32) + outside).astype(BF)
    left = dot(d_ref[...], partner).astype(BF)
    combined_real = (following[:, :n].astype(F32) + dot(left[:, :n], dt_ref[...])).astype(BF)
    combined_imag = (following[:, n:].astype(F32) + dot(left[:, n:], dt_ref[...])).astype(BF)
    combined = jnp.concatenate([combined_real, combined_imag], axis=1)
    right[...] = expanded(combined)

    @pl.loop(0, n // ROWS)
    def _(i):
        rows = pl.ds(pl.multiple_of(i * ROWS, ROWS), ROWS)
        product = dot(c_ref[rows, :], right[...]).astype(BF)
        out[rows, :] = (pack[rows, :].astype(F32) + dot(product, w_ref[...])).astype(BF)


def advance(linked, following, near, far, pack, prepared):
    n = following.shape[0]
    return pl.pallas_call(
        advance_kernel,
        out_shape=jax.ShapeDtypeStruct((n, 2 * n), BF),
        in_specs=[SM] + [VM] * 8,
        out_specs=VM,
        scratch_shapes=[pltpu.VMEM((2 * n, 2 * n), BF)],
        compiler_params=pltpu.CompilerParams(vmem_limit_bytes=24 << 20),
        cost_estimate=pl.CostEstimate(flops=24 * n**3, bytes_accessed=24 * n * n, transcendentals=0),
    )(linked, following, near, far, pack, *prepared)


def after(value, *others):
    return lax.optimization_barrier((value, *others))[0]


def device(x, y, z, core):
    return ((z * 2 + y // 2) * 2 + core) * 8 + (y % 2) * 4 + x


PLACES = ([(3, 1), (3, 2), (3, 0), (3, 3)], [(1, 0), (1, 3), (1, 1), (1, 2)])
SEATS = [[(*place[i % 4], i // 2) for i in range(8)] for place in PLACES]
DEPTH = 5


def make(energies, layers):
    def home(k, l):
        return k * layers + l

    def seat(k, p):
        k %= energies
        return device(*SEATS[p][k // 2], k % 2)

    chip_swap = [(home(k, j), home(k ^ 1, j)) for k in range(energies) for j in range(layers)]
    far_pairs = {}
    for p in range(2):
        for k in range(energies):
            far_pairs[seat(k, p)] = seat(k + 1 if k % 2 else k - 1, p)
    far_pairs = [(s, far_pairs.get(s, d)) for s, d in chip_swap]
    top = layers - 1

    def to_seat(l, p):
        return [(home(k, l), seat(k, p)) for k in range(energies)] if 0 <= l <= top else []

    def to_home(l, p):
        return [(t, s) for s, t in to_seat(l, p)]

    def per_device(green_local, hopping, coupling):
        k = lax.axis_index("energy")
        position = lax.axis_index("layer")
        core = (k % 2).astype(jnp.int32)
        n = hopping.shape[1]
        me = k * layers + position
        ends = [me == seat(e, p) for e in (0, energies - 1) for p in range(2)]
        linked = jnp.where(ends[0] | ends[1] | ends[2] | ends[3], 0, 1).astype(jnp.int32).reshape(1)
        isolated = [green_local[0, p].reshape(n, 2 * n) for p in range(2)]
        coupling_rows = jnp.concatenate([coupling[0, : n // 2], coupling[0, n // 2 :]], axis=1)
        shared = jnp.concatenate([hopping[0].reshape(n, 2 * n), coupling_rows], axis=0)
        half = shared.shape[0] // 2
        my_half = lax.dynamic_slice_in_dim(shared, core * half, half, axis=0)
        core = core.reshape(1)

        def move(value, pairs):
            return lax.ppermute(value, AXES, pairs)

        even = (top - position) % 2 == 0
        first = move(isolated[0], to_seat(top, 0))
        halves = move(my_half, to_seat(top, 0))
        blocks = [jnp.where(even, isolated[0], isolated[1]), jnp.where(even, isolated[1], isolated[0])]
        packs = [jnp.concatenate([b, my_half], axis=0) for b in blocks]
        arrived = {}

        def fetch(s, token):
            pairs = to_seat(top - s, 0) + to_seat(top + 1 - s, 1)
            arrived[s] = move(after(packs[s % 2], token), pairs)

        second_chain = me == seat(0, 1)
        for e in range(1, energies):
            second_chain |= me == seat(e, 1)
        following = first
        fetch(1, my_half)
        for s in range(2, DEPTH):
            fetch(s, first)
        waiting, sums = [[], []], [None, None]
        for s in range(layers + 1):
            if s == 0:
                pack, own = first, halves
            elif s == 1:
                pack = after(arrived.pop(s), following)
                own = pack[n:]
                result_0 = following
                following = jnp.where(second_chain, pack[:n], following)
            else:
                pack = after(arrived.pop(s), following)
                own = pack[n:]
            far = move(following, far_pairs)
            near = move(following, chip_swap)
            if s > 0:
                pairs = to_home(top + 1 - s, 0) + to_home(top + 2 - s, 1)
                waiting[(s - 1) % 2].append(move(result_0 if s == 1 else following, pairs))
            if s + DEPTH <= layers:
                fetch(s + DEPTH, following)
            other = move(own, chip_swap)
            prepared = prepare(core, pack, own, other)
            following = advance(linked, following, near, far, pack, prepared)
            if s > 2:
                i = (s - 1) % 2
                part = after(waiting[i].pop(0), following)
                sums[i] = part if sums[i] is None else sums[i] + part
        waiting[layers % 2].append(move(following, to_home(0, 1)))
        totals = []
        for held, parts in zip(sums, waiting, strict=True):
            for part in parts:
                held = part if held is None else held + part
            totals.append(held)
        result = [jnp.where(even, totals[p], totals[1 - p]) for p in range(2)]
        return jnp.stack([r.reshape(n, 2, n) for r in result])[None]

    return per_device


def solution(mesh):
    placed = (
        P("layer", "energy", None, None, None),
        P("layer", None, None, None),
        P("layer", None, None),
    )
    return jax.shard_map(
        make(mesh.shape["energy"], mesh.shape["layer"]),
        mesh=mesh,
        in_specs=placed,
        out_specs=P("layer", "energy", None, None, None),
        check_vma=False,
    )
```
